32 devices in a mesh: grp: 4 (over x, core), row: 4 (over z), col: 2 (over y).
Axes of the slice: x: 2, y: 2, z: 4, core: 2. Of those that a mesh axis runs over, the one named last changes fastest.
Arguments:
- low_t: float32 [4, 4096, 768], P('grp', ('row', 'col')), may hold values from -8 to 8, as said below
- inv_first: float32 [4, 4096, 4096], P('grp', ('row', 'col')), may hold values from -8 to 8, as said below
- coupling_num: int32 [4, 4096, 4096], P('grp', ('row', 'col')), may hold values from -16 to 16
Outputs:
- solved: float32 [4, 4096, 768], P('grp', ('row', 'col'))
- swapped: float32 [4, 4096, 768], P('grp', ('row', 'col'))
The draws below stay inside these ranges and needn't reach their ends.
Inputs may be any that keep to these rules, and one draw needn't show every extreme that they name: low_t[g, k, i] is zero where k > 3328 + i (rows of a lower-triangular matrix); its entries at k = 3328 + i lie in 0.5 to 2. inv_first[g] is lower triangular with diagonal entries in 0.5 to 2.
All inputs are finite; a program needn't handle non-finite values.
Results may differ from the reference program's by a relative error of at most 0.000071.
Values sent between devices are 32-bit elements; how exact they have to be, the bound alone decides.
A program may use at most 128 MiB of HBM per device.

```python
import math
import jax
import jax.numpy as jnp
from jax import lax

B = 4096
BAND = 6144
ROWS = 768
MERGES = 4


def draw_low_t(key, part):
    key_off, key_diag = jax.random.split(jax.random.fold_in(key, 11), 2)
    depth = jnp.arange(B)[:, None]
    column = jnp.arange(ROWS)[None, :]
    diagonal_at = B - ROWS + column
    off_part = jnp.clip(jax.random.normal(key_off, (MERGES, B, ROWS), jnp.float32), -4.0, 4.0) * (1.5 / math.sqrt(B))
    diag_part = jnp.exp(jax.random.uniform(key_diag, (MERGES, 1, ROWS), jnp.float32, math.log(0.5), math.log(2.0)))
    return jnp.where(depth == diagonal_at, diag_part, jnp.where(depth < diagonal_at, off_part, 0.0)).astype(jnp.float32)


def draw_inv_first(key, part):
    key_off, key_diag = jax.random.split(jax.random.fold_in(key, 23), 2)
    row_index = jnp.arange(B)[:, None]
    col_index = jnp.arange(B)[None, :]
    off_part = jnp.clip(jax.random.normal(key_off, (MERGES, B, B), jnp.float32), -4.0, 4.0) * (1.5 / math.sqrt(B))
    diag_part = jnp.exp(jax.random.uniform(key_diag, (MERGES, B, 1), jnp.float32, math.log(0.5), math.log(2.0)))
    return jnp.where(row_index == col_index, diag_part, jnp.where(col_index < row_index, off_part, 0.0)).astype(jnp.float32)


def plant(drawn, stream_key, least, high):
    index_at = [jax.random.randint(jax.random.fold_in(stream_key, axis), (), 0, length) for axis, length in enumerate(drawn.shape)]
    widest = drawn.shape.index(max(drawn.shape))
    beside = index_at[:widest] + [(index_at[widest] + 1) % drawn.shape[widest]] + index_at[widest + 1:]
    return drawn.at[tuple(index_at)].set(least).at[tuple(beside)].set(high)


def setup_inputs(seed: int = 0) -> dict:
    key_of = jax.random.split(jax.random.key(seed), 4)
    return {
        "low_t": draw_low_t(jax.random.fold_in(key_of[3], 71), 0),
        "inv_first": draw_inv_first(jax.random.fold_in(key_of[3], 71), 0),
        "coupling_num": plant(jax.random.randint(key_of[2], (MERGES, B, B), -16, 17), jax.random.fold_in(key_of[2], 1), -16, 16).astype(jnp.int32),
    }


HIGHEST = lax.Precision.HIGHEST


def reference(low_t, inv_first, coupling_num):
    row_index = jnp.arange(B, dtype=jnp.int32)[:, None]
    col_index = jnp.arange(B, dtype=jnp.int32)[None, :]
    inside = (B + row_index - col_index) <= BAND

    def merge_one(operands):
        low_part, inv_part, num_part = operands
        coupling = jnp.where(inside, num_part.astype(jnp.float32) / 64.0, jnp.float32(0.0))
        product = jnp.dot(coupling.T, low_part, precision=HIGHEST, preferred_element_type=jnp.float32)
        return -jnp.dot(inv_part.T, product, precision=HIGHEST, preferred_element_type=jnp.float32)

    solved = lax.map(merge_one, (low_t, inv_first, coupling_num))
    swapped = solved.reshape(MERGES // 2, 2, B, ROWS)[:, ::-1].reshape(MERGES, B, ROWS)
    return solved, swapped
```

```python
import functools
import jax
import jax.numpy as jnp
from jax import lax
from jax.experimental import pallas as pl
from jax.experimental.pallas import tpu as pltpu
from jax.sharding import PartitionSpec as P

B = 4096
BAND = 6144
CHUNKS = 24
LAGS = (0, 1, 3)
SPLIT = 10
READY = 2
MESH = pl.DeviceIdType.MESH


def loop(count, body):
    def step(i, carry):
        body(i)
        return carry

    lax.fori_loop(0, count, step, 0)


def halves(value):
    high = value.astype(jnp.bfloat16)
    return high, (value - high.astype(jnp.float32)).astype(jnp.bfloat16)


def kernel(
    rows, cols, low_ref, inv_ref, num_ref, out_ref, swap_ref,
    num_tile, inv_tile, coupling, inv_high, inv_low, turned, lhs, acc,
    sendb, own, col_in, row_in, hub_in, hop_in,
    num_sem, inv_sem, col_send, col_recv, row_send, row_recv, hub_send, hub_recv,
    hop_send, hop_recv, swap_send, swap_recv,
):
    chunks, width = own.shape[0], own.shape[2]
    block = low_ref.shape[0]
    group_of = turned.shape[0] // width
    _, tall, total = inv_tile.shape
    tiles = block // tall
    sub = min(16, tall)
    r, c, g = lax.axis_index("row"), lax.axis_index("col"), lax.axis_index("grp")
    group = cols * block
    mate = g + 1 - 2 * lax.rem(g, 2)

    def needed(step, source, target):
        if step == 0:
            return total + source * group - (target + 1) * group + 1 <= BAND
        return target <= source

    final, hub = rows - 1, rows - 2

    def crosses(step, n, source, z, target):
        q, p = r * cols + source, z * cols + target
        if step == 0:
            inside = total + (q - p - 1) * block + 1 <= BAND
            return inside & (q * block < total - (chunks - n - 1) * width)
        return p <= q

    def pooled(source, target):
        return (source == final) & (target < hub) & needed(0, source, target)

    def direct(n):
        return (r == final) & (final > 0) & (n >= SPLIT)

    barrier = pltpu.get_barrier_semaphore()
    peers = [{"grp": mate}]
    peers += [{"col": lax.rem(c + d, cols)} for d in range(1, cols)]
    peers += [{"row": lax.rem(r + d, rows)} for d in range(1, rows)]
    for peer in peers:
        pl.semaphore_signal(barrier, inc=1, device_id=peer, device_id_type=MESH)

    def num_copy(q):
        return pltpu.make_async_copy(
            num_ref.at[:, pl.ds(pl.multiple_of(q * block, block), block)], num_tile.at[q], num_sem.at[q]
        )

    def inv_copy(i):
        slot = lax.rem(i, 2)
        return pltpu.make_async_copy(
            inv_ref.at[pl.ds(pl.multiple_of(i * tall, tall), tall)], inv_tile.at[slot], inv_sem.at[slot]
        )

    def fetch(d):
        def column(z):
            @pl.when(needed(0, r, z))
            def _():
                num_copy(z * cols + lax.rem(c + d, cols)).start()

        loop(rows, column)

    for d in list(range(1, cols)) + [0]:
        fetch(d)
    inv_copy(0).start()

    def convert_num(q):
        num_copy(q).wait()
        high = min(64, block)

        def part(s):
            at = pl.ds(pl.multiple_of(s * high, high), high)
            row = (r * cols + c) * block + s * high + lax.broadcasted_iota(jnp.int32, (high, block), 0)
            col = q * block + lax.broadcasted_iota(jnp.int32, (high, block), 1)
            value = num_tile[q, at, :].astype(jnp.float32) * (1.0 / 64.0)
            value = jnp.where(total + row - col <= BAND, value, 0.0)
            coupling[at, pl.ds(pl.multiple_of(q * block, block), block)] = value.astype(jnp.bfloat16)

        loop(block // high, part)

    def convert_inv(i):
        @pl.when(i + 1 < tiles)
        def _():
            inv_copy(i + 1).start()

        inv_copy(i).wait()
        slot = lax.rem(i, 2)

        def part(s):
            at = pl.ds(pl.multiple_of(s * sub, sub), sub)
            to = pl.ds(pl.multiple_of(i * tall + s * sub, sub), sub)
            high, low = halves(inv_tile[slot, at, :])
            inv_high[to, :] = high
            inv_low[to, :] = low

        loop(tall // sub, part)

    def col_copy(step, n, d, z):
        return pltpu.make_async_remote_copy(
            src_ref=sendb.at[n, d - 1, z],
            dst_ref=col_in.at[step, n, d - 1, z],
            send_sem=col_send.at[step, n, d - 1, z],
            recv_sem=col_recv.at[step, n, d - 1, z],
            device_id={"col": lax.rem(c + d, cols)},
            device_id_type=MESH,
        )

    def row_copy(n, d):
        target = lax.rem(r + d, rows)
        return pltpu.make_async_remote_copy(
            src_ref=own.at[n, target],
            dst_ref=row_in.at[n, d - 1],
            send_sem=row_send.at[n, d - 1],
            recv_sem=row_recv.at[n, d - 1],
            device_id={"row": target},
            device_id_type=MESH,
        )

    def hub_copy(n, z):
        return pltpu.make_async_remote_copy(
            src_ref=own.at[n, z],
            dst_ref=hub_in.at[n, z],
            send_sem=hub_send.at[n, z],
            recv_sem=hub_recv.at[n, z],
            device_id={"row": lax.rem(r + rows - 1, rows)},
            device_id_type=MESH,
        )

    def hop_copy(n, slot, source):
        return pltpu.make_async_remote_copy(
            src_ref=source,
            dst_ref=hop_in.at[n, slot],
            send_sem=hop_send.at[n, slot],
            recv_sem=hop_recv.at[n, slot],
            device_id={"row": lax.rem(r + rows - 1, rows)},
            device_id_type=MESH,
        )

    def far_copy(n, d):
        return hop_copy(n, rows - 2 + d, sendb.at[n, d - 1, 0])

    def near_copy(n, z):
        return hop_copy(n, z, own.at[n, z])

    def lanes(b):
        return pl.ds(pl.multiple_of(b * turned.shape[0], turned.shape[0]), turned.shape[0])

    def swap_copy(b):
        return pltpu.make_async_remote_copy(
            src_ref=out_ref.at[:, lanes(b)],
            dst_ref=swap_ref.at[:, lanes(b)],
            send_sem=swap_send.at[b],
            recv_sem=swap_recv.at[b],
            device_id={"grp": mate},
            device_id_type=MESH,
        )

    def term(step, owner):
        at = pl.ds(pl.multiple_of(owner * block, block), block)
        right = coupling if step == 0 else inv_high
        both = jnp.dot(lhs[...], right[:, at], preferred_element_type=jnp.float32)
        result = both[:width] + both[width:]
        if step == 1:
            result += jnp.dot(lhs[:width], inv_low[:, at], preferred_element_type=jnp.float32)
        return result

    def form(step, n, value):
        high, low = halves(value)
        lhs[:width] = high
        lhs[width:] = low

        def ready(q):
            if step == 0:
                @pl.when(n == 0)
                def _():
                    convert_num(q)

        def wanted(z, d):
            target = lax.rem(c + d, cols)
            if step == 0:
                return crosses(0, n, c, z, target)
            return (z == 0) | crosses(1, n, c, z, target)

        def turn(i):
            return rows - 1 - i if step == 0 else i

        def away(i):
            z, before = turn(i), turn(i - 1)

            @pl.when((i < rows) & needed(step, r, z))
            def _():
                for d in range(1, cols):
                    owner = z * cols + lax.rem(c + d, cols)
                    ready(owner)

                    @pl.when(wanted(z, d))
                    def _():
                        sendb[n, d - 1, z] = term(step, owner)

            @pl.when((i > 0) & needed(step, r, before))
            def _():
                for d in range(1, cols):
                    go = wanted(before, d)
                    if step == 1:
                        go = go & ((before > 0) | direct(n))

                    @pl.when(go)
                    def _():
                        col_copy(step, n, d, before).start()

        def home(i):
            z = turn(i)

            @pl.when(needed(step, r, z))
            def _():
                ready(z * cols + c)
                own[n, z] = term(step, z * cols + c)

        loop(rows + 1, away)
        loop(rows, home)

    def held(target):
        return (r == hub) & pooled(final, target)

    def join(n):
        def add(z):
            @pl.when(needed(0, r, z))
            def _():
                for d in range(1, cols):
                    @pl.when(crosses(0, n, lax.rem(c + cols - d, cols), z, c))
                    def _():
                        col_copy(0, n, d, z).wait_recv()
                        own[n, z] += col_in[0, n, d - 1, z]

        loop(rows, add)
        for target in reversed(range(rows)):
            @pl.when((target != r) & needed(0, r, target) & ~pooled(r, target) & ~held(target))
            def _():
                row_copy(n, lax.rem(target - r + rows, rows)).start()

        for z in range(hub):
            @pl.when(pooled(r, z))
            def _():
                hub_copy(n, z).start()

    def pool(n):
        for z in range(hub):
            @pl.when(held(z))
            def _():
                hub_copy(n, z).wait_recv()
                own[n, z] += hub_in[n, z]

        for z in range(hub):
            @pl.when(held(z))
            def _():
                row_copy(n, z - hub + rows).start()

    def middle(n):
        acc[...] = own[n, r]
        for d in range(1, rows):
            source = lax.rem(r + rows - d, rows)

            @pl.when(needed(0, source, r) & ~pooled(source, r))
            def _():
                row_copy(n, d).wait_recv()
                acc[...] += row_in[n, d - 1]
        for d in range(1, rows):
            target = lax.rem(r + d, rows)

            @pl.when(needed(0, r, target) & ~pooled(r, target))
            def _():
                row_copy(n, d).wait_send()
        for z in range(hub):
            @pl.when(pooled(r, z))
            def _():
                hub_copy(n, z).wait_send()

        def sent(z):
            @pl.when(needed(0, r, z))
            def _():
                for d in range(1, cols):
                    @pl.when(crosses(0, n, c, z, lax.rem(c + d, cols)))
                    def _():
                        col_copy(0, n, d, z).wait_send()

        loop(rows, sent)
        form(1, n, acc[...])

    above, below = r < final, r > 0

    def spread(n):
        return ~((r + 1 == final) & (n >= SPLIT))

    def relay(n):
        @pl.when(direct(n))
        def _():
            for d in range(1, cols):
                col_copy(1, n, d, 0).wait_recv()
                own[n, 0] += col_in[1, n, d - 1, 0]

        @pl.when(above)
        def _():
            near_copy(n, 0).wait_recv()
            own[n, 0] += hop_in[n, 0]

        @pl.when(above & spread(n))
        def _():
            for d in range(1, cols):
                far_copy(n, d).wait_recv()
                sendb[n, d - 1, 0] += hop_in[n, rows - 2 + d]

        @pl.when(below)
        def _():
            near_copy(n, 0).start()

        @pl.when(below & ~direct(n))
        def _():
            for d in range(1, cols):
                far_copy(n, d).start()

        @pl.when(r == 0)
        def _():
            for d in range(1, cols):
                col_copy(1, n, d, 0).start()

        for z in range(1, rows):
            @pl.when(z <= r)
            def _():
                for d in range(1, cols):
                    @pl.when(crosses(1, n, lax.rem(c + cols - d, cols), z, c))
                    def _():
                        col_copy(1, n, d, z).wait_recv()
                        own[n, z] += col_in[1, n, d - 1, z]

            if z < rows - 1:
                @pl.when((z <= r) & above)
                def _():
                    near_copy(n, z).wait_recv()
                    own[n, z] += hop_in[n, z]

                @pl.when(z < r)
                def _():
                    near_copy(n, z).start()

    def last(n):
        @pl.when(r == 0)
        def _():
            for d in range(1, cols):
                col_copy(1, n, d, 0).wait_recv()
                own[n, 0] += col_in[1, n, d - 1, 0]

        @pl.when(lax.rem(n, group_of) == group_of - 1)
        def _():
            b = lax.div(n, group_of)
            piece = own[pl.ds(n - (group_of - 1), group_of), r]
            out_ref[:, lanes(b)] = -piece.reshape(group_of * width, block).T
            swap_copy(b).start()

    def settle(n):
        for d in range(1, cols):
            @pl.when((r == 0) | direct(n))
            def _():
                col_copy(1, n, d, 0).wait_send()

            @pl.when(below & ~direct(n))
            def _():
                far_copy(n, d).wait_send()

        for z in range(rows):
            if z > 0:
                for d in range(1, cols):
                    @pl.when((z <= r) & crosses(1, n, c, z, lax.rem(c + d, cols)))
                    def _():
                        col_copy(1, n, d, z).wait_send()

            if z < rows - 1:
                @pl.when(z < r)
                def _():
                    near_copy(n, z).wait_send()

        @pl.when(lax.rem(n, group_of) == 0)
        def _():
            swap_copy(lax.div(n, group_of)).wait()

    pl.semaphore_wait(barrier, len(peers))

    def stage(t, lag, body):
        n = t - lag

        @pl.when((n >= 0) & (n < chunks))
        def _():
            body(n)

    def pipeline(t):
        @pl.when((t < chunks) & (lax.rem(t, group_of) == 0))
        def _():
            turned[...] = low_ref[:, lanes(lax.div(t, group_of))].T

        def head(n):
            at = pl.multiple_of(lax.rem(n, group_of) * width, width)
            form(0, n, turned[pl.ds(at, width)])

        stage(t, LAGS[0], head)

        stage(t, LAGS[1], join)

        @pl.when(t == READY)
        def _():
            loop(tiles, convert_inv)

        if hub > 0:
            @pl.when((r == hub) & pooled(final, hub - 1))
            def _():
                stage(t, LAGS[2], pool)

            late = (r <= hub) & pooled(final, jnp.minimum(r, hub - 1))
            stage(t, LAGS[2] + jnp.where(late, 1, 0), middle)
        else:
            stage(t, LAGS[2], middle)
        lag = LAGS[2] + rows - r
        stage(t, lag, relay)
        stage(t, lag + jnp.where(r == 0, 1, 0), last)

    loop(chunks + LAGS[2] + rows + 1, pipeline)
    loop(chunks, settle)


def local(low_t, inv_first, coupling_num):
    rows, cols = lax.axis_size("row"), lax.axis_size("col")
    _, block, width = low_t.shape
    total = inv_first.shape[2]
    chunk = width // CHUNKS
    turn = 128
    tiles = 8
    tall = block // tiles
    vmem = functools.partial(pl.BlockSpec, memory_space=pltpu.VMEM)
    hbm = functools.partial(pl.BlockSpec, memory_space=pl.ANY)
    dma = pltpu.SemaphoreType.DMA
    piece = (chunk, block)
    hops = rows + cols - 2
    result = jax.ShapeDtypeStruct((block, width), jnp.float32)
    solved, swapped = pl.pallas_call(
        functools.partial(kernel, rows, cols),
        out_shape=(result, result),
        in_specs=[vmem(), hbm(), hbm()],
        out_specs=(vmem(), hbm()),
        scratch_shapes=[
            pltpu.VMEM((rows * cols, block, block), jnp.int32),
            pltpu.VMEM((2, tall, total), jnp.float32),
            pltpu.VMEM((block, total), jnp.bfloat16),
            pltpu.VMEM((block, total), jnp.bfloat16),
            pltpu.VMEM((block, total), jnp.bfloat16),
            pltpu.VMEM((turn, block), jnp.float32),
            pltpu.VMEM((2 * chunk, block), jnp.bfloat16),
            pltpu.VMEM(piece, jnp.float32),
            pltpu.VMEM((CHUNKS, cols - 1, rows) + piece, jnp.float32),
            pltpu.VMEM((CHUNKS, rows) + piece, jnp.float32),
            pltpu.VMEM((2, CHUNKS, cols - 1, rows) + piece, jnp.float32),
            pltpu.VMEM((CHUNKS, rows - 1) + piece, jnp.float32),
            pltpu.VMEM((CHUNKS, rows - 2) + piece, jnp.float32),
            pltpu.VMEM((CHUNKS, hops) + piece, jnp.float32),
            dma((rows * cols,)),
            dma((2,)),
            dma((2, CHUNKS, cols - 1, rows)),
            dma((2, CHUNKS, cols - 1, rows)),
            dma((CHUNKS, rows - 1)),
            dma((CHUNKS, rows - 1)),
            dma((CHUNKS, rows - 2)),
            dma((CHUNKS, rows - 2)),
            dma((CHUNKS, hops)),
            dma((CHUNKS, hops)),
            dma((width // turn,)),
            dma((width // turn,)),
        ],
        compiler_params=pltpu.CompilerParams(
            collective_id=0, has_side_effects=True, vmem_limit_bytes=67043328
        ),
    )(low_t[0], inv_first[0], coupling_num[0])
    return solved[None], swapped[None]


def solution(mesh):
    placed = (
        P("grp", ("row", "col"), None),
        P("grp", ("row", "col"), None),
        P("grp", ("row", "col"), None),
    )
    return jax.shard_map(
        local,
        mesh=mesh,
        in_specs=placed,
        out_specs=(P("grp", ("row", "col"), None), P("grp", ("row", "col"), None)),
        check_vma=False,
    )
```

```python
import functools
import jax
import jax.numpy as jnp
from jax import lax
from jax.experimental import pallas as pl
from jax.experimental.pallas import tpu as pltpu
from jax.sharding import PartitionSpec as P

B = 4096
BAND = 6144
CHUNKS = 24
LAGS = (0, 1, 3)
SPLIT = 10
READY = 2
PAUSE = 3
MESH = pl.DeviceIdType.MESH


def loop(count, body):
    def step(i, carry):
        body(i)
        return carry

    lax.fori_loop(0, count, step, 0)


def halves(value):
    high = value.astype(jnp.bfloat16)
    return high, (value - high.astype(jnp.float32)).astype(jnp.bfloat16)


def kernel(
    rows, cols, low_ref, inv_ref, num_ref, out_ref, swap_ref,
    num_tile, inv_tile, coupling, inv_high, inv_low, turned, lhs, acc,
    sendb, own, col_in, row_in, hub_in, hop_in,
    num_sem, inv_sem, col_send, col_recv, row_send, row_recv, hub_send, hub_recv,
    hop_send, hop_recv, swap_send, swap_recv,
):
    chunks, width = own.shape[0], own.shape[2]
    block = low_ref.shape[0]
    group_of = turned.shape[0] // width
    _, tall, total = inv_tile.shape
    tiles = block // tall
    sub = min(16, tall)
    r, c, g = lax.axis_index("row"), lax.axis_index("col"), lax.axis_index("grp")
    group = cols * block
    mate = g + 1 - 2 * lax.rem(g, 2)

    def needed(step, source, target):
        if step == 0:
            return total + source * group - (target + 1) * group + 1 <= BAND
        return target <= source

    final, hub = rows - 1, rows - 2
    cut = max(1, rows // 2)

    def crosses(step, n, source, z, target):
        q, p = r * cols + source, z * cols + target
        if step == 0:
            inside = total + (q - p - 1) * block + 1 <= BAND
            return inside & (q * block < total - (chunks - n - 1) * width)
        return p <= q

    def pooled(source, target):
        return (source == final) & (target < hub) & needed(0, source, target)

    def direct(n):
        return (r == final) & (final > 0) & (n >= SPLIT)

    barrier = pltpu.get_barrier_semaphore()
    peers = [{"grp": mate}]
    peers += [{"col": lax.rem(c + d, cols)} for d in range(1, cols)]
    peers += [{"row": lax.rem(r + d, rows)} for d in range(1, rows)]
    for peer in peers:
        pl.semaphore_signal(barrier, inc=1, device_id=peer, device_id_type=MESH)

    def num_copy(q):
        return pltpu.make_async_copy(
            num_ref.at[:, pl.ds(pl.multiple_of(q * block, block), block)], num_tile.at[q], num_sem.at[q]
        )

    def inv_copy(i):
        slot = lax.rem(i, 2)
        return pltpu.make_async_copy(
            inv_ref.at[pl.ds(pl.multiple_of(i * tall, tall), tall)], inv_tile.at[slot], inv_sem.at[slot]
        )

    def fetch(d):
        def column(z):
            @pl.when(needed(0, r, z))
            def _():
                num_copy(z * cols + lax.rem(c + d, cols)).start()

        loop(rows, column)

    for d in list(range(1, cols)) + [0]:
        fetch(d)
    inv_copy(0).start()

    def convert_num(q):
        num_copy(q).wait()
        high = min(64, block)

        def part(s):
            at = pl.ds(pl.multiple_of(s * high, high), high)
            row = (r * cols + c) * block + s * high + lax.broadcasted_iota(jnp.int32, (high, block), 0)
            col = q * block + lax.broadcasted_iota(jnp.int32, (high, block), 1)
            value = num_tile[q, at, :].astype(jnp.float32) * (1.0 / 64.0)
            value = jnp.where(total + row - col <= BAND, value, 0.0)
            coupling[at, pl.ds(pl.multiple_of(q * block, block), block)] = value.astype(jnp.bfloat16)

        loop(block // high, part)

    def convert_inv(i):
        @pl.when(i + 1 < tiles)
        def _():
            inv_copy(i + 1).start()

        inv_copy(i).wait()
        slot = lax.rem(i, 2)

        def part(s):
            at = pl.ds(pl.multiple_of(s * sub, sub), sub)
            to = pl.ds(pl.multiple_of(i * tall + s * sub, sub), sub)
            high, low = halves(inv_tile[slot, at, :])
            inv_high[to, :] = high
            inv_low[to, :] = low

        loop(tall // sub, part)

    def col_copy(step, n, d, z, count=1):
        return pltpu.make_async_remote_copy(
            src_ref=sendb.at[n, d - 1, pl.ds(z, count)],
            dst_ref=col_in.at[step, n, d - 1, pl.ds(z, count)],
            send_sem=col_send.at[step, n, d - 1, z],
            recv_sem=col_recv.at[step, n, d - 1, z],
            device_id={"col": lax.rem(c + d, cols)},
            device_id_type=MESH,
        )

    def span(step, n, d, sending, act, begin=0, end=rows):
        source, target = (c, lax.rem(c + d, cols)) if sending else (lax.rem(c + cols - d, cols), c)
        first = jnp.where(direct(n), 0, 1) if step == 1 and begin == 0 else begin
        length = 0
        for z in range(begin, end):
            length = length + jnp.where(crosses(step, n, source, z, target) & (z >= first), 1, 0)
        for count in range(1, end - begin + 1):
            @pl.when(length == count)
            def _():
                act(col_copy(step, n, d, first if step == 1 else rows - count, count))

    def row_copy(n, d):
        target = lax.rem(r + d, rows)
        return pltpu.make_async_remote_copy(
            src_ref=own.at[n, target],
            dst_ref=row_in.at[n, d - 1],
            send_sem=row_send.at[n, d - 1],
            recv_sem=row_recv.at[n, d - 1],
            device_id={"row": target},
            device_id_type=MESH,
        )

    def hub_copy(n, z):
        return pltpu.make_async_remote_copy(
            src_ref=own.at[n, z],
            dst_ref=hub_in.at[n, z],
            send_sem=hub_send.at[n, z],
            recv_sem=hub_recv.at[n, z],
            device_id={"row": lax.rem(r + rows - 1, rows)},
            device_id_type=MESH,
        )

    def hop_copy(n, slot, source):
        return pltpu.make_async_remote_copy(
            src_ref=source,
            dst_ref=hop_in.at[n, slot],
            send_sem=hop_send.at[n, slot],
            recv_sem=hop_recv.at[n, slot],
            device_id={"row": lax.rem(r + rows - 1, rows)},
            device_id_type=MESH,
        )

    def far_copy(n, d):
        return hop_copy(n, rows - 2 + d, sendb.at[n, d - 1, 0])

    def near_copy(n, z):
        return hop_copy(n, z, own.at[n, z])

    def lanes(b):
        return pl.ds(pl.multiple_of(b * turned.shape[0], turned.shape[0]), turned.shape[0])

    def swap_copy(b):
        return pltpu.make_async_remote_copy(
            src_ref=out_ref.at[:, lanes(b)],
            dst_ref=swap_ref.at[:, lanes(b)],
            send_sem=swap_send.at[b],
            recv_sem=swap_recv.at[b],
            device_id={"grp": mate},
            device_id_type=MESH,
        )

    def term(step, owner):
        at = pl.ds(pl.multiple_of(owner * block, block), block)
        right = coupling if step == 0 else inv_high
        both = jnp.dot(lhs[...], right[:, at], preferred_element_type=jnp.float32)
        result = both[:width] + both[width:]
        if step == 1:
            result += jnp.dot(lhs[:width], inv_low[:, at], preferred_element_type=jnp.float32)
        return result

    def form(step, n, value, begin=0, end=rows):
        high, low = halves(value)
        lhs[:width] = high
        lhs[width:] = low

        def ready(q):
            if step == 0:
                @pl.when(n == 0)
                def _():
                    convert_num(q)

        def wanted(z, d):
            target = lax.rem(c + d, cols)
            if step == 0:
                return crosses(0, n, c, z, target)
            return (z == 0) | crosses(1, n, c, z, target)

        def turn(i):
            return rows - 1 - i if step == 0 else begin + i

        def away(i):
            z = turn(i)

            @pl.when(needed(step, r, z))
            def _():
                for d in range(1, cols):
                    owner = z * cols + lax.rem(c + d, cols)
                    ready(owner)

                    @pl.when(wanted(z, d))
                    def _():
                        sendb[n, d - 1, z] = term(step, owner)

        def home(i):
            z = turn(i)

            @pl.when(needed(step, r, z))
            def _():
                ready(z * cols + c)
                own[n, z] = term(step, z * cols + c)

        loop(end - begin, away)
        home(0)
        for d in range(1, cols):
            span(step, n, d, True, lambda copy: copy.start(), begin, end)
        if end - begin > 1:
            loop(end - begin - 1, lambda i: home(i + 1))

    def held(target):
        return (r == hub) & pooled(final, target)

    def join(n):
        for d in range(1, cols):
            span(0, n, d, False, lambda copy: copy.wait_recv())

        def add(z):
            @pl.when(needed(0, r, z))
            def _():
                for d in range(1, cols):
                    @pl.when(crosses(0, n, lax.rem(c + cols - d, cols), z, c))
                    def _():
                        own[n, z] += col_in[0, n, d - 1, z]

        loop(rows, add)
        for target in reversed(range(rows)):
            @pl.when((target != r) & needed(0, r, target) & ~pooled(r, target) & ~held(target))
            def _():
                row_copy(n, lax.rem(target - r + rows, rows)).start()

        for z in range(hub):
            @pl.when(pooled(r, z))
            def _():
                hub_copy(n, z).start()

    def pool(n):
        for z in range(hub):
            @pl.when(held(z))
            def _():
                hub_copy(n, z).wait_recv()
                own[n, z] += hub_in[n, z]

        for z in range(hub):
            @pl.when(held(z))
            def _():
                row_copy(n, z - hub + rows).start()

    def middle(n):
        acc[...] = own[n, r]
        for d in range(1, rows):
            source = lax.rem(r + rows - d, rows)

            @pl.when(needed(0, source, r) & ~pooled(source, r))
            def _():
                row_copy(n, d).wait_recv()
                acc[...] += row_in[n, d - 1]
        for d in range(1, rows):
            target = lax.rem(r + d, rows)

            @pl.when(needed(0, r, target) & ~pooled(r, target))
            def _():
                row_copy(n, d).wait_send()
        for z in range(hub):
            @pl.when(pooled(r, z))
            def _():
                hub_copy(n, z).wait_send()

        for d in range(1, cols):
            span(0, n, d, True, lambda copy: copy.wait_send())
        own[n, r] = acc[...]
        form(1, n, acc[...], 0, cut)

    def middle_rest(n):
        form(1, n, own[n, r], cut, rows)

    above, below = r < final, r > 0

    def spread(n):
        return ~((r + 1 == final) & (n >= SPLIT))

    def relay(n):
        @pl.when(above & spread(n))
        def _():
            for d in range(1, cols):
                far_copy(n, d).wait_recv()
                sendb[n, d - 1, 0] += hop_in[n, rows - 2 + d]

        @pl.when(below & ~direct(n))
        def _():
            for d in range(1, cols):
                far_copy(n, d).start()

        @pl.when(r == 0)
        def _():
            for d in range(1, cols):
                col_copy(1, n, d, 0).start()

        def gather():
            for d in range(1, cols):
                span(1, n, d, False, lambda copy: copy.wait_recv(), 0, cut)

        @pl.when(direct(n))
        def _():
            gather()
            for d in range(1, cols):
                own[n, 0] += col_in[1, n, d - 1, 0]

        @pl.when(above)
        def _():
            near_copy(n, 0).wait_recv()
            own[n, 0] += hop_in[n, 0]

        @pl.when(below)
        def _():
            near_copy(n, 0).start()

        @pl.when(~direct(n))
        def _():
            gather()

        carry(n, 1, cut)

    def relay_rest(n):
        for d in range(1, cols):
            span(1, n, d, False, lambda copy: copy.wait_recv(), cut, rows)
        carry(n, cut, rows)

    def carry(n, begin, end):
        for z in range(begin, end):
            @pl.when(z <= r)
            def _():
                for d in range(1, cols):
                    @pl.when(crosses(1, n, lax.rem(c + cols - d, cols), z, c))
                    def _():
                        own[n, z] += col_in[1, n, d - 1, z]

            if z < rows - 1:
                @pl.when((z <= r) & above)
                def _():
                    near_copy(n, z).wait_recv()
                    own[n, z] += hop_in[n, z]

                @pl.when(z < r)
                def _():
                    near_copy(n, z).start()

    def last(n):
        @pl.when(r == 0)
        def _():
            for d in range(1, cols):
                col_copy(1, n, d, 0).wait_recv()
                own[n, 0] += col_in[1, n, d - 1, 0]

        @pl.when(lax.rem(n, group_of) == group_of - 1)
        def _():
            b = lax.div(n, group_of)
            piece = own[pl.ds(n - (group_of - 1), group_of), r]
            out_ref[:, lanes(b)] = piece.reshape(group_of * width, block).T
            swap_copy(b).start()

    def settle(n):
        for d in range(1, cols):
            span(1, n, d, True, lambda copy: copy.wait_send(), 0, cut)
            if cut < rows:
                span(1, n, d, True, lambda copy: copy.wait_send(), cut, rows)

            @pl.when(r == 0)
            def _():
                col_copy(1, n, d, 0).wait_send()

            @pl.when(below & ~direct(n))
            def _():
                far_copy(n, d).wait_send()

        for z in range(rows):
            if z < rows - 1:
                @pl.when(z < r)
                def _():
                    near_copy(n, z).wait_send()

        @pl.when(lax.rem(n, group_of) == 0)
        def _():
            swap_copy(lax.div(n, group_of)).wait()

    pl.semaphore_wait(barrier, len(peers))

    def stage(t, lag, body):
        n = t - lag

        @pl.when((n >= 0) & (n < chunks))
        def _():
            body(n)

    def pipeline(t):
        @pl.when((t < chunks) & (lax.rem(t, group_of) == 0))
        def _():
            turned[...] = low_ref[:, lanes(lax.div(t, group_of))].T

        def head(n):
            at = pl.multiple_of(lax.rem(n, group_of) * width, width)
            form(0, n, turned[pl.ds(at, width)])

        stage(t, LAGS[0], head)

        stage(t, LAGS[1], join)

        @pl.when(t == READY)
        def _():
            loop(tiles, convert_inv)

        late = 0
        if hub > 0:
            @pl.when((r == hub) & pooled(final, hub - 1))
            def _():
                stage(t, LAGS[2], pool)

            late = jnp.where((r <= hub) & pooled(final, jnp.minimum(r, hub - 1)), 1, 0)
        lag = LAGS[2] + rows - r
        rest = jnp.where(r >= cut, PAUSE, 0)
        stage(t, LAGS[2] + late, middle)
        if cut < rows:
            @pl.when(r >= cut)
            def _():
                stage(t, LAGS[2] + late + rest, middle_rest)

        stage(t, lag, relay)
        if cut < rows:
            @pl.when(r >= cut)
            def _():
                stage(t, lag + rest, relay_rest)

        stage(t, lag + jnp.where(r == 0, 1, 0) + rest, last)

    loop(chunks + LAGS[2] + rows + 1 + PAUSE, pipeline)
    loop(chunks, settle)


def local(low_t, inv_first, coupling_num):
    rows, cols = lax.axis_size("row"), lax.axis_size("col")
    _, block, width = low_t.shape
    total = inv_first.shape[2]
    chunk = width // CHUNKS
    turn = 128
    tiles = 8
    tall = block // tiles
    vmem = functools.partial(pl.BlockSpec, memory_space=pltpu.VMEM)
    hbm = functools.partial(pl.BlockSpec, memory_space=pl.ANY)
    dma = pltpu.SemaphoreType.DMA
    piece = (chunk, block)
    hops = rows + cols - 2
    result = jax.ShapeDtypeStruct((block, width), jnp.float32)
    solved, swapped = pl.pallas_call(
        functools.partial(kernel, rows, cols),
        out_shape=(result, result),
        in_specs=[vmem(), hbm(), hbm()],
        out_specs=(vmem(), hbm()),
        scratch_shapes=[
            pltpu.VMEM((rows * cols, block, block), jnp.int32),
            pltpu.VMEM((2, tall, total), jnp.float32),
            pltpu.VMEM((block, total), jnp.bfloat16),
            pltpu.VMEM((block, total), jnp.bfloat16),
            pltpu.VMEM((block, total), jnp.bfloat16),
            pltpu.VMEM((turn, block), jnp.float32),
            pltpu.VMEM((2 * chunk, block), jnp.bfloat16),
            pltpu.VMEM(piece, jnp.float32),
            pltpu.VMEM((CHUNKS, cols - 1, rows) + piece, jnp.float32),
            pltpu.VMEM((CHUNKS, rows) + piece, jnp.float32),
            pltpu.VMEM((2, CHUNKS, cols - 1, rows) + piece, jnp.float32),
            pltpu.VMEM((CHUNKS, rows - 1) + piece, jnp.float32),
            pltpu.VMEM((CHUNKS, rows - 2) + piece, jnp.float32),
            pltpu.VMEM((CHUNKS, hops) + piece, jnp.float32),
            dma((rows * cols,)),
            dma((2,)),
            dma((2, CHUNKS, cols - 1, rows)),
            dma((2, CHUNKS, cols - 1, rows)),
            dma((CHUNKS, rows - 1)),
            dma((CHUNKS, rows - 1)),
            dma((CHUNKS, rows - 2)),
            dma((CHUNKS, rows - 2)),
            dma((CHUNKS, hops)),
            dma((CHUNKS, hops)),
            dma((width // turn,)),
            dma((width // turn,)),
        ],
        compiler_params=pltpu.CompilerParams(
            collective_id=0, has_side_effects=True, vmem_limit_bytes=67043328
        ),
    )(low_t[0], inv_first[0], coupling_num[0])
    return -solved[None], -swapped[None]


def solution(mesh):
    placed = (
        P("grp", ("row", "col"), None),
        P("grp", ("row", "col"), None),
        P("grp", ("row", "col"), None),
    )
    return jax.shard_map(
        local,
        mesh=mesh,
        in_specs=placed,
        out_specs=(P("grp", ("row", "col"), None), P("grp", ("row", "col"), None)),
        check_vma=False,
    )
```

```python
import functools
import jax
import jax.numpy as jnp
from jax import lax
from jax.experimental import pallas as pl
from jax.experimental.pallas import tpu as pltpu
from jax.sharding import PartitionSpec as P

B = 4096
BAND = 6144
CHUNKS = 24
LAGS = (0, 1, 3)
SPLIT = 10
READY = 2
PAUSE = 3
MESH = pl.DeviceIdType.MESH


def loop(count, body):
    def step(i, carry):
        body(i)
        return carry

    lax.fori_loop(0, count, step, 0)


def halves(value):
    high = value.astype(jnp.bfloat16)
    return high, (value - high.astype(jnp.float32)).astype(jnp.bfloat16)


def kernel(
    rows, cols, low_ref, inv_ref, num_ref, out_ref, swap_ref,
    num_tile, inv_tile, coupling, inv_high, inv_low, turned, lhs, acc,
    sendb, own, col_in, row_in, hub_in, hop_in,
    num_sem, inv_sem, col_send, col_recv, row_send, row_recv, hub_send, hub_recv,
    hop_send, hop_recv, swap_send, swap_recv,
):
    chunks, width = own.shape[0], own.shape[2]
    block = low_ref.shape[0]
    group_of = turned.shape[0] // width
    _, tall, total = inv_tile.shape
    tiles = block // tall
    sub = min(16, tall)
    r, c, g = lax.axis_index("row"), lax.axis_index("col"), lax.axis_index("grp")
    group = cols * block
    mate = g + 1 - 2 * lax.rem(g, 2)

    def needed(step, source, target):
        if step == 0:
            return total + source * group - (target + 1) * group + 1 <= BAND
        return target <= source

    final, hub = rows - 1, rows - 2
    cut = max(1, rows // 2)

    def crosses(step, n, source, z, target):
        q, p = r * cols + source, z * cols + target
        if step == 0:
            inside = total + (q - p - 1) * block + 1 <= BAND
            return inside & (q * block < total - (chunks - n - 1) * width)
        return p <= q

    def pooled(source, target):
        return (source == final) & (target < hub) & needed(0, source, target)

    def direct(n):
        return (r == final) & (final > 0) & (n >= SPLIT)

    barrier = pltpu.get_barrier_semaphore()
    peers = [{"grp": mate}]
    peers += [{"col": lax.rem(c + d, cols)} for d in range(1, cols)]
    peers += [{"row": lax.rem(r + d, rows)} for d in range(1, rows)]
    for peer in peers:
        pl.semaphore_signal(barrier, inc=1, device_id=peer, device_id_type=MESH)

    def num_copy(q):
        return pltpu.make_async_copy(
            num_ref.at[:, pl.ds(pl.multiple_of(q * block, block), block)], num_tile.at[q], num_sem.at[q]
        )

    def inv_copy(i):
        slot = lax.rem(i, 2)
        return pltpu.make_async_copy(
            inv_ref.at[pl.ds(pl.multiple_of(i * tall, tall), tall)], inv_tile.at[slot], inv_sem.at[slot]
        )

    def fetch(d):
        def column(z):
            @pl.when(needed(0, r, z))
            def _():
                num_copy(z * cols + lax.rem(c + d, cols)).start()

        loop(rows, column)

    for d in list(range(1, cols)) + [0]:
        fetch(d)
    inv_copy(0).start()

    def convert_num(q):
        num_copy(q).wait()
        high = min(64, block)

        def part(s):
            at = pl.ds(pl.multiple_of(s * high, high), high)
            row = (r * cols + c) * block + s * high + lax.broadcasted_iota(jnp.int32, (high, block), 0)
            col = q * block + lax.broadcasted_iota(jnp.int32, (high, block), 1)
            value = num_tile[q, at, :].astype(jnp.float32) * (1.0 / 64.0)
            value = jnp.where(total + row - col <= BAND, value, 0.0)
            coupling[at, pl.ds(pl.multiple_of(q * block, block), block)] = value.astype(jnp.bfloat16)

        loop(block // high, part)

    def convert_inv(i):
        @pl.when(i + 1 < tiles)
        def _():
            inv_copy(i + 1).start()

        inv_copy(i).wait()
        slot = lax.rem(i, 2)

        def part(s):
            at = pl.ds(pl.multiple_of(s * sub, sub), sub)
            to = pl.ds(pl.multiple_of(i * tall + s * sub, sub), sub)
            high, low = halves(inv_tile[slot, at, :])
            inv_high[to, :] = high
            inv_low[to, :] = low

        loop(tall // sub, part)

    def col_copy(step, n, d, z, count=1):
        return pltpu.make_async_remote_copy(
            src_ref=sendb.at[n, d - 1, pl.ds(z, count)],
            dst_ref=col_in.at[step, n, d - 1, pl.ds(z, count)],
            send_sem=col_send.at[step, n, d - 1, z],
            recv_sem=col_recv.at[step, n, d - 1, z],
            device_id={"col": lax.rem(c + d, cols)},
            device_id_type=MESH,
        )

    def span(step, n, d, sending, act, begin=0, end=rows):
        source, target = (c, lax.rem(c + d, cols)) if sending else (lax.rem(c + cols - d, cols), c)
        first = jnp.where(direct(n), 0, 1) if step == 1 and begin == 0 else begin
        length = 0
        for z in range(begin, end):
            length = length + jnp.where(crosses(step, n, source, z, target) & (z >= first), 1, 0)
        for count in range(1, end - begin + 1):
            @pl.when(length == count)
            def _():
                act(col_copy(step, n, d, first if step == 1 else rows - count, count))

    def row_copy(n, d):
        target = lax.rem(r + d, rows)
        return pltpu.make_async_remote_copy(
            src_ref=own.at[n, target],
            dst_ref=row_in.at[n, d - 1],
            send_sem=row_send.at[n, d - 1],
            recv_sem=row_recv.at[n, d - 1],
            device_id={"row": target},
            device_id_type=MESH,
        )

    def hub_copy(n, z):
        return pltpu.make_async_remote_copy(
            src_ref=own.at[n, z],
            dst_ref=hub_in.at[n, z],
            send_sem=hub_send.at[n, z],
            recv_sem=hub_recv.at[n, z],
            device_id={"row": lax.rem(r + rows - 1, rows)},
            device_id_type=MESH,
        )

    def hop_copy(n, slot, source):
        return pltpu.make_async_remote_copy(
            src_ref=source,
            dst_ref=hop_in.at[n, slot],
            send_sem=hop_send.at[n, slot],
            recv_sem=hop_recv.at[n, slot],
            device_id={"row": lax.rem(r + rows - 1, rows)},
            device_id_type=MESH,
        )

    def far_copy(n, d):
        return hop_copy(n, rows - 2 + d, sendb.at[n, d - 1, 0])

    def near_copy(n, z):
        return hop_copy(n, z, own.at[n, z])

    def lanes(b):
        return pl.ds(pl.multiple_of(b * turned.shape[0], turned.shape[0]), turned.shape[0])

    def swap_copy(b):
        return pltpu.make_async_remote_copy(
            src_ref=out_ref.at[:, lanes(b)],
            dst_ref=swap_ref.at[:, lanes(b)],
            send_sem=swap_send.at[b],
            recv_sem=swap_recv.at[b],
            device_id={"grp": mate},
            device_id_type=MESH,
        )

    def term(step, owner):
        at = pl.ds(pl.multiple_of(owner * block, block), block)
        right = coupling if step == 0 else inv_high
        both = jnp.dot(lhs[...], right[:, at], preferred_element_type=jnp.float32)
        result = both[:width] + both[width:]
        if step == 1:
            result += jnp.dot(lhs[:width], inv_low[:, at], preferred_element_type=jnp.float32)
        return result

    def form(step, n, value, begin=0, end=rows):
        high, low = halves(value)
        lhs[:width] = high
        lhs[width:] = low

        def ready(q):
            if step == 0:
                @pl.when(n == 0)
                def _():
                    convert_num(q)

        def wanted(z, d):
            target = lax.rem(c + d, cols)
            if step == 0:
                return crosses(0, n, c, z, target)
            return (z == 0) | crosses(1, n, c, z, target)

        def turn(i):
            return rows - 1 - i if step == 0 else begin + i

        def away(i):
            z = turn(i)

            @pl.when(needed(step, r, z))
            def _():
                for d in range(1, cols):
                    owner = z * cols + lax.rem(c + d, cols)
                    ready(owner)

                    @pl.when(wanted(z, d))
                    def _():
                        sendb[n, d - 1, z] = term(step, owner)

        def home(i):
            z = turn(i)

            @pl.when(needed(step, r, z))
            def _():
                ready(z * cols + c)
                own[n, z] = term(step, z * cols + c)

        loop(end - begin, away)
        home(0)
        for d in range(1, cols):
            span(step, n, d, True, lambda copy: copy.start(), begin, end)
        if end - begin > 1:
            loop(end - begin - 1, lambda i: home(i + 1))

    def held(target):
        return (r == hub) & pooled(final, target)

    def join(n):
        for d in range(1, cols):
            span(0, n, d, False, lambda copy: copy.wait_recv())

        def add(z):
            @pl.when(needed(0, r, z))
            def _():
                for d in range(1, cols):
                    @pl.when(crosses(0, n, lax.rem(c + cols - d, cols), z, c))
                    def _():
                        own[n, z] += col_in[0, n, d - 1, z]

        loop(rows, add)
        for target in reversed(range(rows)):
            @pl.when((target != r) & needed(0, r, target) & ~pooled(r, target) & ~held(target))
            def _():
                row_copy(n, lax.rem(target - r + rows, rows)).start()

        for z in range(hub):
            @pl.when(pooled(r, z))
            def _():
                hub_copy(n, z).start()

    def pool(n):
        for z in range(hub):
            @pl.when(held(z))
            def _():
                hub_copy(n, z).wait_recv()
                own[n, z] += hub_in[n, z]

        for z in range(hub):
            @pl.when(held(z))
            def _():
                row_copy(n, z - hub + rows).start()

    def middle(n):
        acc[...] = own[n, r]
        for d in range(1, rows):
            source = lax.rem(r + rows - d, rows)

            @pl.when(needed(0, source, r) & ~pooled(source, r))
            def _():
                row_copy(n, d).wait_recv()
                acc[...] += row_in[n, d - 1]
        for d in range(1, rows):
            target = lax.rem(r + d, rows)

            @pl.when(needed(0, r, target) & ~pooled(r, target))
            def _():
                row_copy(n, d).wait_send()
        for z in range(hub):
            @pl.when(pooled(r, z))
            def _():
                hub_copy(n, z).wait_send()

        for d in range(1, cols):
            span(0, n, d, True, lambda copy: copy.wait_send())
        own[n, r] = acc[...]
        form(1, n, acc[...], 0, cut)

        @pl.when((r == final) & (r > 0) & ~direct(n))
        def _():
            for d in range(1, cols):
                far_copy(n, d).start()

    def middle_rest(n):
        form(1, n, own[n, r], cut, rows)

    above, below = r < final, r > 0

    def spread(n):
        return ~((r + 1 == final) & (n >= SPLIT))

    def relay(n):
        @pl.when(above & spread(n))
        def _():
            for d in range(1, cols):
                far_copy(n, d).wait_recv()
                sendb[n, d - 1, 0] += hop_in[n, rows - 2 + d]

        @pl.when(below & (r < final))
        def _():
            for d in range(1, cols):
                far_copy(n, d).start()

        @pl.when(r == 0)
        def _():
            for d in range(1, cols):
                col_copy(1, n, d, 0).start()

        def gather():
            for d in range(1, cols):
                span(1, n, d, False, lambda copy: copy.wait_recv(), 0, cut)

        @pl.when(direct(n))
        def _():
            gather()
            for d in range(1, cols):
                own[n, 0] += col_in[1, n, d - 1, 0]

        @pl.when(above)
        def _():
            near_copy(n, 0).wait_recv()
            own[n, 0] += hop_in[n, 0]

        @pl.when(below)
        def _():
            near_copy(n, 0).start()

        @pl.when(~direct(n))
        def _():
            gather()

        carry(n, 1, cut)

    def relay_rest(n):
        for d in range(1, cols):
            span(1, n, d, False, lambda copy: copy.wait_recv(), cut, rows)
        carry(n, cut, rows)

    def carry(n, begin, end):
        for z in range(begin, end):
            @pl.when(z <= r)
            def _():
                for d in range(1, cols):
                    @pl.when(crosses(1, n, lax.rem(c + cols - d, cols), z, c))
                    def _():
                        own[n, z] += col_in[1, n, d - 1, z]

            if z < rows - 1:
                @pl.when((z <= r) & above)
                def _():
                    near_copy(n, z).wait_recv()
                    own[n, z] += hop_in[n, z]

                @pl.when(z < r)
                def _():
                    near_copy(n, z).start()

    def last(n):
        @pl.when(r == 0)
        def _():
            for d in range(1, cols):
                col_copy(1, n, d, 0).wait_recv()
                own[n, 0] += col_in[1, n, d - 1, 0]

        @pl.when(lax.rem(n, group_of) == group_of - 1)
        def _():
            b = lax.div(n, group_of)
            piece = own[pl.ds(n - (group_of - 1), group_of), r]
            out_ref[:, lanes(b)] = piece.reshape(group_of * width, block).T
            swap_copy(b).start()

    def settle(n):
        for d in range(1, cols):
            span(1, n, d, True, lambda copy: copy.wait_send(), 0, cut)
            if cut < rows:
                span(1, n, d, True, lambda copy: copy.wait_send(), cut, rows)

            @pl.when(r == 0)
            def _():
                col_copy(1, n, d, 0).wait_send()

            @pl.when(below & ~direct(n))
            def _():
                far_copy(n, d).wait_send()

        for z in range(rows):
            if z < rows - 1:
                @pl.when(z < r)
                def _():
                    near_copy(n, z).wait_send()

        @pl.when(lax.rem(n, group_of) == 0)
        def _():
            swap_copy(lax.div(n, group_of)).wait()

    pl.semaphore_wait(barrier, len(peers))

    def stage(t, lag, body):
        n = t - lag

        @pl.when((n >= 0) & (n < chunks))
        def _():
            body(n)

    def pipeline(t):
        @pl.when((t < chunks) & (lax.rem(t, group_of) == 0))
        def _():
            turned[...] = low_ref[:, lanes(lax.div(t, group_of))].T

        def head(n):
            at = pl.multiple_of(lax.rem(n, group_of) * width, width)
            form(0, n, turned[pl.ds(at, width)])

        stage(t, LAGS[0], head)

        stage(t, LAGS[1], join)

        @pl.when(t == READY)
        def _():
            loop(tiles, convert_inv)

        late = 0
        if hub > 0:
            @pl.when((r == hub) & pooled(final, hub - 1))
            def _():
                stage(t, LAGS[2], pool)

            late = jnp.where((r <= hub) & pooled(final, jnp.minimum(r, hub - 1)), 1, 0)
        lag = LAGS[2] + rows - r
        rest = jnp.where(r >= cut, PAUSE, 0)
        stage(t, LAGS[2] + late, middle)
        if cut < rows:
            @pl.when(r >= cut)
            def _():
                stage(t, LAGS[2] + late + rest, middle_rest)

        stage(t, lag, relay)
        if cut < rows:
            @pl.when(r >= cut)
            def _():
                stage(t, lag + rest, relay_rest)

        stage(t, lag + jnp.where(r == 0, 1, 0) + rest, last)

    loop(chunks + LAGS[2] + rows + 1 + PAUSE, pipeline)
    loop(chunks, settle)


def local(low_t, inv_first, coupling_num):
    rows, cols = lax.axis_size("row"), lax.axis_size("col")
    _, block, width = low_t.shape
    total = inv_first.shape[2]
    chunk = width // CHUNKS
    turn = 128
    tiles = 8
    tall = block // tiles
    vmem = functools.partial(pl.BlockSpec, memory_space=pltpu.VMEM)
    hbm = functools.partial(pl.BlockSpec, memory_space=pl.ANY)
    dma = pltpu.SemaphoreType.DMA
    piece = (chunk, block)
    hops = rows + cols - 2
    result = jax.ShapeDtypeStruct((block, width), jnp.float32)
    solved, swapped = pl.pallas_call(
        functools.partial(kernel, rows, cols),
        out_shape=(result, result),
        in_specs=[vmem(), hbm(), hbm()],
        out_specs=(vmem(), hbm()),
        scratch_shapes=[
            pltpu.VMEM((rows * cols, block, block), jnp.int32),
            pltpu.VMEM((2, tall, total), jnp.float32),
            pltpu.VMEM((block, total), jnp.bfloat16),
            pltpu.VMEM((block, total), jnp.bfloat16),
            pltpu.VMEM((block, total), jnp.bfloat16),
            pltpu.VMEM((turn, block), jnp.float32),
            pltpu.VMEM((2 * chunk, block), jnp.bfloat16),
            pltpu.VMEM(piece, jnp.float32),
            pltpu.VMEM((CHUNKS, cols - 1, rows) + piece, jnp.float32),
            pltpu.VMEM((CHUNKS, rows) + piece, jnp.float32),
            pltpu.VMEM((2, CHUNKS, cols - 1, rows) + piece, jnp.float32),
            pltpu.VMEM((CHUNKS, rows - 1) + piece, jnp.float32),
            pltpu.VMEM((CHUNKS, rows - 2) + piece, jnp.float32),
            pltpu.VMEM((CHUNKS, hops) + piece, jnp.float32),
            dma((rows * cols,)),
            dma((2,)),
            dma((2, CHUNKS, cols - 1, rows)),
            dma((2, CHUNKS, cols - 1, rows)),
            dma((CHUNKS, rows - 1)),
            dma((CHUNKS, rows - 1)),
            dma((CHUNKS, rows - 2)),
            dma((CHUNKS, rows - 2)),
            dma((CHUNKS, hops)),
            dma((CHUNKS, hops)),
            dma((width // turn,)),
            dma((width // turn,)),
        ],
        compiler_params=pltpu.CompilerParams(
            collective_id=0, has_side_effects=True, vmem_limit_bytes=67043328
        ),
    )(low_t[0], inv_first[0], coupling_num[0])
    return -solved[None], -swapped[None]


def solution(mesh):
    placed = (
        P("grp", ("row", "col"), None),
        P("grp", ("row", "col"), None),
        P("grp", ("row", "col"), None),
    )
    return jax.shard_map(
        local,
        mesh=mesh,
        in_specs=placed,
        out_specs=(P("grp", ("row", "col"), None), P("grp", ("row", "col"), None)),
        check_vma=False,
    )
```
